32 devices in a mesh: dp: 2 (over y), row: 4 (over z), col: 4 (over x, core).
Axes of the slice: x: 2, y: 2, z: 4, core: 2. Of those that a mesh axis runs over, the one named last changes fastest.
Arguments:
- inputs: bfloat16 [4, 2420736], P('row', ('dp', 'col')), may hold values from -32 to 32
- live_images: int32 [2], P('dp'), may hold values from 1 to 32, 40 in all
- w_qkv: bfloat16 [3, 768, 768], P(None, 'row', 'col'), may hold values from -4 to 4
- qv_bias: float32 [2, 768], P(None, 'col'), may hold values from -3 to 3
- w_out: bfloat16 [768, 768], P('col', 'row'), may hold values from -0.625 to 0.625
- out_bias: float32 [768], P('row'), may hold values from -3 to 3
- attention_norm_gain: float32 [768], P('row'), may hold values from 0.5 to 1.5
- attention_norm_bias: float32 [768], P('row'), may hold values from -3 to 3
- feedforward_norm_gain: float32 [768], P('row'), may hold values from 0.5 to 1.5
- feedforward_norm_bias: float32 [768], P('row'), may hold values from -3 to 3
- w_up: bfloat16 [768, 3072], P('row', 'col'), may hold values from -0.21875 to 0.21875
- up_bias: float32 [3072], P('col'), may hold values from -3 to 3
- w_down: bfloat16 [768, 3072], P('row', 'col'), may hold values from -0.15625 to 0.15625
- down_bias: float32 [768], P('row'), may hold values from -3 to 3
- cotangent: bfloat16 [4, 2420736], P('row', ('dp', 'col')), may hold values from -6 to 6
Outputs:
- result: float32 [4, 2420736], P('row', ('dp', 'col'))
- input_gradient: float32 [4, 2420736], P('row', ('dp', 'col'))
- grad_qkv: float32 [3, 768, 768], P(None, 'row', 'col')
- grad_qvbias: float32 [2, 768], P(None, 'col')
- output_weight_gradient: float32 [768, 768], P('col', 'row')
- grad_outbias: float32 [768], P('row')
- grad_gainattn: float32 [768], P('row')
- grad_shiftattn: float32 [768], P('row')
- grad_gainmlp: float32 [768], P('row')
- grad_shiftmlp: float32 [768], P('row')
- up_weight_gradient: float32 [768, 3072], P('row', 'col')
- grad_upbias: float32 [3072], P('col')
- down_weight_gradient: float32 [768, 3072], P('row', 'col')
- grad_downbias: float32 [768], P('row')
The draws below stay inside these ranges and needn't reach their ends.
Inputs may be any that keep to these rules, and one draw needn't show every extreme that they name: Data group g holds live_images[g] real images in its first slots.
All inputs are finite; a program needn't handle non-finite values.
Results may differ from the reference program's by a relative error of at most 0.012.
Values may be sent and summed in bfloat16 or wider, within the bound.
A program may use at most 192 MiB of HBM per device.

```python
import math
import jax
import jax.numpy as jnp
import numpy as np
from jax import lax

D = 768
H = 12
HD = 64
FF = 3072
S = 197
CAP = 32
IMAGES = 64
N_DP = 2
N_ROW = 4


def draw_inputs(key, part):
    key_a, key_b, key_c = jax.random.split(key, 3)
    noise = jnp.clip(jax.random.normal(key_a, (IMAGES, S, D), jnp.float32), -4.0, 4.0) * 0.5
    row_scale = jnp.exp(jax.random.uniform(key_b, (IMAGES, S, 1), jnp.float32, math.log(0.3), math.log(3.0)))
    ramp = jnp.arange(D).astype(jnp.float32) / (D - 1)
    col_scale = jnp.exp(ramp * math.log(3.0) + jax.random.uniform(key_c, (D,), jnp.float32, -0.3, 0.3))
    tokens = noise * row_scale * col_scale
    folded = tokens.reshape(IMAGES, S, N_ROW, D // N_ROW).transpose(2, 0, 1, 3).reshape(N_ROW, IMAGES * S * (D // N_ROW))
    return folded.astype(jnp.bfloat16)


def draw_w_qkv(key, part):
    key_a = jax.random.fold_in(key, 0)
    noise = jnp.clip(jax.random.normal(key_a, (3, D, D), jnp.float32), -4.0, 4.0) / math.sqrt(D)
    return noise.astype(jnp.bfloat16)


def block_levels(rng, extent, shards, low, top_value):
    gain = 1.0
    for position, parts in shards:
        steps = jax.random.uniform(jax.random.fold_in(jax.random.fold_in(rng, 6), position), (parts,), jnp.float32, low / len(shards), top_value / len(shards))
        gain = gain * jnp.repeat(jnp.exp(steps), extent[position] // parts).reshape((-1,) + (1,) * (len(extent) - 1 - position))
    return gain


def length_profile(amount, total, limit, lean):
    portions = [(1 << 20) // math.isqrt(grade ** lean) + 1 for grade in range(2, amount + 1)]
    rest, counts = total - limit - (amount - 1), [1] * (amount - 1)
    while rest > 0:
        free = [i for i in range(amount - 1) if counts[i] < limit]
        whole, left = sum([portions[i] for i in free]), rest
        for i in free:
            more = min(limit - counts[i], max(1, left * portions[i] // whole), rest)
            counts[i] = counts[i] + more
            rest = rest - more
    return np.array([limit] + counts)


def uneven(key, number_of, total, most, skew):
    if number_of == 2:
        one = jax.random.randint(key, (), max(1, total - most), min(most, total - 1) + 1)
        return jnp.stack([one, total - one])
    lengths = jnp.asarray(length_profile(number_of, total, most, skew), jnp.int32)
    couples = (number_of - 1) // 2
    donor, sink = lengths[1:1 + 2 * couples:2], lengths[2:2 + 2 * couples:2]
    slack = jnp.minimum(donor - 1, most - sink)
    passed = jax.random.randint(jax.random.fold_in(key, 1), (couples,), 0, 1 << 20) % (slack + 1)
    lengths = lengths.at[1:1 + 2 * couples:2].set(donor - passed).at[2:2 + 2 * couples:2].set(sink + passed)
    return lengths[jax.random.permutation(jax.random.fold_in(key, 2), number_of)]


def bell_draw(rng, shape, scale, most, shards=(), dtype=jnp.bfloat16):
    values = jax.random.normal(rng, shape, jnp.float32) * scale
    if len(shards) > 0:
        values = block_levels(rng, shape, shards, -0.22, 0.18) * values
    return jnp.clip(values, min=-most, max=most).astype(dtype)


def setup_inputs(seed: int = 0) -> dict:
    seeds = jax.random.split(jax.random.key(seed), 16)
    return {
        "inputs": draw_inputs(jax.random.fold_in(seeds[15], 71), 0),
        "live_images": uneven(seeds[1], N_DP, N_DP * CAP * 5 // 8, CAP, 2).astype(jnp.int32),
        "w_qkv": draw_w_qkv(jax.random.fold_in(seeds[15], 71), 0),
        "qv_bias": bell_draw(seeds[3], (2, D), 0.5, 3.0, ((1, 4),), jnp.float32),
        "w_out": bell_draw(seeds[4], (D, D), (D // 8) ** -0.5, 0.625, ((0, 4), (1, 4))),
        "out_bias": bell_draw(seeds[5], (D,), 0.5, 3.0, ((0, 4),), jnp.float32),
        "attention_norm_gain": jnp.clip(1.0 + 0.1 * jax.random.normal(seeds[6], (D,), jnp.float32), 0.5, 1.5),
        "attention_norm_bias": bell_draw(seeds[7], (D,), 0.5, 3.0, ((0, 4),), jnp.float32),
        "feedforward_norm_gain": jnp.clip(1.0 + 0.1 * jax.random.normal(seeds[8], (D,), jnp.float32), 0.5, 1.5),
        "feedforward_norm_bias": bell_draw(seeds[9], (D,), 0.5, 3.0, ((0, 4),), jnp.float32),
        "w_up": bell_draw(seeds[10], (D, FF), D ** -0.5, 0.21875, ((0, 4), (1, 4))),
        "up_bias": bell_draw(seeds[11], (FF,), 0.5, 3.0, ((0, 4),), jnp.float32),
        "w_down": bell_draw(seeds[12], (D, FF), (FF // 2) ** -0.5, 0.15625, ((0, 4), (1, 4))),
        "down_bias": bell_draw(seeds[13], (D,), 0.5, 3.0, ((0, 4),), jnp.float32),
        "cotangent": bell_draw(seeds[14], (N_ROW, IMAGES * S * D // N_ROW), 1.0, 6.0, ((0, 4), (1, 8))),
    }


EPS = 1e-06
ROOT_HALF = 0.7071067811865476
INV_ROOT_TAU = 0.3989422804014327

def rounded(features):
    return lax.optimization_barrier(features.astype(jnp.bfloat16)).astype(jnp.float32)

def gelu_value(preact):
    return 0.5 * preact * (1.0 + lax.erf(preact * ROOT_HALF))

def gelu_slope(preact):
    return 0.5 * (1.0 + lax.erf(preact * ROOT_HALF)) + preact * jnp.exp(-0.5 * preact * preact) * INV_ROOT_TAU

def layer_norm_apply(features, gain_vec, shift_vec):
    average = lax.optimization_barrier(jnp.mean(features, -1, keepdims=True))
    inv_std = lax.rsqrt(lax.optimization_barrier(jnp.mean(features * features, -1, keepdims=True)) - average * average + EPS)
    centred = (features - average) * inv_std
    return (centred, inv_std, (centred * gain_vec + shift_vec).astype(jnp.bfloat16))

def layer_norm_backprop(grad_normed, centred, inv_std, gain_vec):
    scaled = grad_normed * gain_vec
    plain_term = lax.optimization_barrier(jnp.mean(scaled, -1, keepdims=True))
    second = lax.optimization_barrier(jnp.mean(scaled * centred, -1, keepdims=True))
    return inv_std * (scaled - plain_term - centred * second)

def dot32(left, right):
    return jnp.dot(left, right, preferred_element_type=jnp.float32)

def unfold_tokens(flat):
    return flat.reshape(N_ROW, IMAGES, S, D // N_ROW).transpose(1, 2, 0, 3).reshape(IMAGES, S, D)

def fold_tokens(tokens):
    return tokens.reshape(IMAGES, S, N_ROW, D // N_ROW).transpose(2, 0, 1, 3).reshape(N_ROW, IMAGES * S * (D // N_ROW))

def one_group(weights, group_data):
    w_qkv, qv_bias, w_out, out_bias, attention_norm_gain, attention_norm_bias, feedforward_norm_gain, feedforward_norm_bias, w_up, up_bias, w_down, down_bias = weights
    inputs, cotangent, live = group_data
    row_count = CAP * S
    scaling = 1.0 / math.sqrt(HD)
    residual_stream = inputs.astype(jnp.float32).reshape(row_count, D)
    first_standardized, first_reciprocal_deviation, first_normalized = layer_norm_apply(residual_stream, attention_norm_gain, attention_norm_bias)
    queries = (dot32(first_normalized, w_qkv[0]) + qv_bias[0]).astype(jnp.bfloat16)
    key_part = dot32(first_normalized, w_qkv[1]).astype(jnp.bfloat16)
    values = (dot32(first_normalized, w_qkv[2]) + qv_bias[1]).astype(jnp.bfloat16)
    query_h = lax.optimization_barrier(queries).astype(jnp.float32).reshape(CAP, S, H, HD)
    key_h = lax.optimization_barrier(key_part).astype(jnp.float32).reshape(CAP, S, H, HD)
    value_h = lax.optimization_barrier(values).astype(jnp.float32).reshape(CAP, S, H, HD)
    scores = jnp.einsum('bqhe,bkhe->bhqk', query_h, key_h) * scaling
    row_max = lax.optimization_barrier(jnp.max(scores, -1, keepdims=True))
    log_total = row_max + jnp.log(lax.optimization_barrier(jnp.sum(jnp.exp(scores - row_max), -1, keepdims=True)))
    prob = jnp.exp(scores - log_total)
    probf = rounded(prob)
    attended = jnp.einsum('bhqk,bkhe->bqhe', probf, value_h).astype(jnp.bfloat16).reshape(row_count, D)
    hidden_state = residual_stream + dot32(attended, w_out) + out_bias
    second_standardized, second_reciprocal_deviation, second_normalized = layer_norm_apply(hidden_state, feedforward_norm_gain, feedforward_norm_bias)
    preact = dot32(second_normalized, w_up) + up_bias
    activation = gelu_value(preact).astype(jnp.bfloat16)
    result = hidden_state + dot32(activation, w_down.T) + down_bias
    alive_rows = (jnp.arange(CAP) < live).astype(jnp.float32)
    layer_output_gradient = (cotangent.astype(jnp.float32) * alive_rows[:, None, None]).reshape(row_count, D)
    grad_yb = layer_output_gradient.astype(jnp.bfloat16)
    down_weight_gradient = dot32(grad_yb.T, activation)
    preactivation_gradient = dot32(grad_yb, w_down) * gelu_slope(preact)
    grad_preb = preactivation_gradient.astype(jnp.bfloat16)
    up_weight_gradient = dot32(second_normalized.T, grad_preb)
    second_normalized_gradient = dot32(grad_preb, w_up.T)
    hidden_gradient = layer_output_gradient + layer_norm_backprop(second_normalized_gradient, second_standardized, second_reciprocal_deviation, feedforward_norm_gain)
    grad_hiddenb = hidden_gradient.astype(jnp.bfloat16)
    output_weight_gradient = dot32(attended.T, grad_hiddenb)
    grad_att = dot32(grad_hiddenb, w_out.T).astype(jnp.bfloat16)
    grad_out_h = lax.optimization_barrier(grad_att).astype(jnp.float32).reshape(CAP, S, H, HD)
    attended_h = lax.optimization_barrier(attended).astype(jnp.float32).reshape(CAP, S, H, HD)
    row_dot = jnp.einsum('bqhe,bqhe->bhq', grad_out_h, attended_h)
    grad_prob = jnp.einsum('bqhe,bkhe->bhqk', grad_out_h, value_h)
    grad_scores = rounded(prob * (grad_prob - row_dot[..., None]))
    grad_query = jnp.einsum('bhqk,bkhe->bqhe', grad_scores, key_h) * scaling
    grad_key = jnp.einsum('bhqk,bqhe->bkhe', grad_scores, query_h) * scaling
    grad_value = jnp.einsum('bhqk,bqhe->bkhe', probf, grad_out_h)
    activation_gradient = jnp.stack([grad_query, grad_key, grad_value], 0).reshape(3, row_count, D)
    grad_actsb = activation_gradient.astype(jnp.bfloat16)
    query_key_value_weight_gradient = jnp.stack([dot32(first_normalized.T, grad_actsb[0]), dot32(first_normalized.T, grad_actsb[1]), dot32(first_normalized.T, grad_actsb[2])], 0)
    first_normalized_gradient = dot32(grad_actsb[0], w_qkv[0].T) + dot32(grad_actsb[1], w_qkv[1].T) + dot32(grad_actsb[2], w_qkv[2].T)
    input_gradient = hidden_gradient + layer_norm_backprop(first_normalized_gradient, first_standardized, first_reciprocal_deviation, attention_norm_gain)
    gradient_bundle = (query_key_value_weight_gradient, jnp.stack([lax.optimization_barrier(jnp.sum(activation_gradient[0], 0)), lax.optimization_barrier(jnp.sum(activation_gradient[2], 0))], 0), output_weight_gradient, lax.optimization_barrier(jnp.sum(hidden_gradient, 0)), lax.optimization_barrier(jnp.sum(first_normalized_gradient * first_standardized, 0)), lax.optimization_barrier(jnp.sum(first_normalized_gradient, 0)), lax.optimization_barrier(jnp.sum(second_normalized_gradient * second_standardized, 0)), lax.optimization_barrier(jnp.sum(second_normalized_gradient, 0)), up_weight_gradient, lax.optimization_barrier(jnp.sum(preactivation_gradient, 0)), down_weight_gradient, lax.optimization_barrier(jnp.sum(layer_output_gradient, 0)))
    return (gradient_bundle, (result.reshape(CAP, S, D), input_gradient.reshape(CAP, S, D)))

def reference(inputs, live_images, w_qkv, qv_bias, w_out, out_bias, attention_norm_gain, attention_norm_bias, feedforward_norm_gain, feedforward_norm_bias, w_up, up_bias, w_down, down_bias, cotangent):
    weights = (w_qkv, qv_bias, w_out, out_bias, attention_norm_gain, attention_norm_bias, feedforward_norm_gain, feedforward_norm_bias, w_up, up_bias, w_down, down_bias)
    initial = tuple((jnp.zeros(weight.shape, jnp.float32) for weight in weights))

    def scan_step(totals, group_data):
        gradient_bundle, outputs = one_group(weights, group_data)
        return (jax.tree.map(jnp.add, totals, gradient_bundle), outputs)
    tokens = unfold_tokens(inputs)
    cotangent_tokens = unfold_tokens(cotangent)
    groups = (tokens.reshape(N_DP, CAP, S, D), cotangent_tokens.reshape(N_DP, CAP, S, D), live_images.astype(jnp.int32))
    totals, outputs = lax.scan(scan_step, initial, groups)
    result = fold_tokens(outputs[0].reshape(IMAGES, S, D))
    input_gradient = fold_tokens(outputs[1].reshape(IMAGES, S, D))
    return (result, input_gradient, totals[0], totals[1], totals[2], totals[3], totals[4], totals[5], totals[6], totals[7], totals[8], totals[9], totals[10], totals[11])
```

```python
import math

import jax
import jax.numpy as jnp
from jax import lax
from jax.sharding import PartitionSpec as P

D = 768
HD = 64
FF = 3072
S = 197


EPS = 1e-06
ROOT_HALF = 0.7071067811865476
INV_ROOT_TAU = 0.3989422804014327


def gelu_value(preact):
    return 0.5 * preact * (1.0 + lax.erf(preact * ROOT_HALF))


def gelu_slope(preact):
    return (
        0.5 * (1.0 + lax.erf(preact * ROOT_HALF))
        + preact * jnp.exp(-0.5 * preact * preact) * INV_ROOT_TAU
    )


def norm_apply(features, gain_vec, shift_vec):
    average = jnp.sum(features, -1, keepdims=True) / D
    squares = jnp.sum(features * features, -1, keepdims=True) / D
    inv_std = lax.rsqrt(squares - average * average + EPS)
    centred = (features - average) * inv_std
    return (centred, inv_std, (centred * gain_vec + shift_vec).astype(jnp.bfloat16))


def norm_backprop(grad_normed, centred, inv_std, gain_vec):
    scaled = grad_normed * gain_vec
    totals = jnp.sum(scaled, -1, keepdims=True) / D
    mixture = jnp.sum(scaled * centred, -1, keepdims=True) / D
    return inv_std * (scaled - totals - centred * mixture)


def dot(spec, left, right):
    return jnp.einsum(spec, left, right, preferred_element_type=jnp.float32)


def gather_weight(block):
    both = lax.all_gather(block, ("col", "row"), axis=0)
    n_col, n_row = lax.axis_size("col"), lax.axis_size("row")
    return both.reshape(n_col, n_row * block.shape[0], block.shape[1])


def scatter_grad(grad):
    part = lax.psum_scatter(grad.astype(jnp.bfloat16), "col", scatter_dimension=0)
    part = lax.psum_scatter(part, "row", scatter_dimension=0, tiled=True)
    if lax.axis_size("dp") == 2:
        other = lax.ppermute(part, "dp", [(0, 1), (1, 0)])
        return part.astype(jnp.float32) + other.astype(jnp.float32)
    return lax.psum(part.astype(jnp.float32), "dp")


def to_rows(flat, own, width_rows):
    tokens = flat.reshape(-1, S, width_rows)
    moved = lax.all_to_all(tokens, "row", split_axis=0, concat_axis=2, tiled=True)
    return moved.reshape(own * S, D)


def from_rows(values, own):
    moved = lax.all_to_all(
        values.astype(jnp.bfloat16).reshape(own, S, D),
        "row",
        split_axis=2,
        concat_axis=0,
        tiled=True,
    )
    return moved.astype(jnp.float32).reshape(1, -1)


def per_device(
    inputs,
    live_images,
    w_qkv,
    qv_bias,
    w_out,
    out_bias,
    attention_norm_gain,
    attention_norm_bias,
    feedforward_norm_gain,
    feedforward_norm_bias,
    w_up,
    up_bias,
    w_down,
    down_bias,
    cotangent,
):
    scaling = 1.0 / math.sqrt(HD)
    n_row, n_col = lax.axis_size("row"), lax.axis_size("col")
    row_idx, col_idx = lax.axis_index("row"), lax.axis_index("col")
    width_rows = D // n_row
    col_width = qv_bias.shape[1]
    col_hidden = up_bias.shape[0]
    heads = col_width // HD
    local_images = inputs.shape[1] // (S * width_rows)
    own = local_images // n_row
    rows = own * S

    tokens = to_rows(inputs, own, width_rows).astype(jnp.float32)
    w_attn = jnp.concatenate(
        [w_qkv.transpose(1, 0, 2).reshape(width_rows, 3 * col_width), w_out.T], 1
    )
    vectors = jnp.concatenate(
        [
            out_bias,
            attention_norm_gain,
            attention_norm_bias,
            feedforward_norm_gain,
            feedforward_norm_bias,
            down_bias,
            qv_bias.reshape(-1),
            up_bias,
        ]
    )
    vectors = lax.all_gather(vectors, ("col", "row"), axis=0).reshape(n_col, n_row, -1)
    row_vecs = vectors[0, :, : 6 * width_rows].reshape(n_row, 6, width_rows)
    row_vecs = row_vecs.transpose(1, 0, 2).reshape(6, D)
    out_b, gain1, shift1, gain2, shift2, down_b = [row_vecs[i] for i in range(6)]
    col_vecs = vectors[:, 0, 6 * width_rows :]
    q_bias = col_vecs[:, :col_width]
    v_bias = col_vecs[:, col_width : 2 * col_width]
    up_b = col_vecs[:, 2 * col_width :]

    wa = gather_weight(w_attn)
    wu = gather_weight(w_up)
    wd = gather_weight(w_down)
    w_in, w_o = wa[:, :, : 3 * col_width], wa[:, :, 3 * col_width :]

    cot = to_rows(cotangent, own, width_rows).astype(jnp.float32)
    first_image = col_idx * local_images + row_idx * own
    alive = (first_image + jnp.arange(own) < live_images[0]).astype(jnp.float32)
    grad_y = (cot.reshape(own, S, D) * alive[:, None, None]).reshape(rows, D)
    grad_yb = grad_y.astype(jnp.bfloat16)

    xhat1, rstd1, normed1 = norm_apply(tokens, gain1, shift1)
    qkv_bias = jnp.concatenate([q_bias, jnp.zeros_like(q_bias), v_bias], 1)
    qkv = (dot("td,cdn->ctn", normed1, w_in) + qkv_bias[:, None, :]).astype(jnp.bfloat16)
    qkv = qkv.reshape(n_col, own, S, 3, heads, HD).transpose(3, 0, 1, 4, 2, 5)
    queries, keys, values = [qkv[i].reshape(n_col * own * heads, S, HD) for i in range(3)]
    scores = dot("bqe,bke->bqk", queries, keys) * scaling
    row_max = jnp.max(scores, -1, keepdims=True)
    log_total = row_max + jnp.log(jnp.sum(jnp.exp(scores - row_max), -1, keepdims=True))
    prob = jnp.exp(scores - log_total)
    probb = prob.astype(jnp.bfloat16)
    attended_h = dot("bqk,bke->bqe", probb, values).astype(jnp.bfloat16)

    def merge(per_head):
        out = per_head.reshape(n_col, own, heads, S, HD).transpose(0, 1, 3, 2, 4)
        return out.reshape(n_col, rows, col_width)

    attended = merge(attended_h)
    hidden = tokens + dot("ctn,cdn->td", attended, w_o) + out_b
    xhat2, rstd2, normed2 = norm_apply(hidden, gain2, shift2)
    preact = dot("td,cdf->ctf", normed2, wu) + up_b[:, None, :]
    activ = gelu_value(preact).astype(jnp.bfloat16)
    result = hidden + dot("ctf,cdf->td", activ, wd) + down_b
    result_out = from_rows(result, own)

    g_down = scatter_grad(dot("td,ctf->cdf", grad_yb, activ))
    grad_pre = dot("td,cdf->ctf", grad_yb, wd) * gelu_slope(preact)
    grad_preb = grad_pre.astype(jnp.bfloat16)
    g_up = scatter_grad(dot("td,ctf->cdf", normed2, grad_preb))
    grad_n2 = dot("ctf,cdf->td", grad_preb, wu)
    grad_hidden = grad_y + norm_backprop(grad_n2, xhat2, rstd2, gain2)
    grad_hiddenb = grad_hidden.astype(jnp.bfloat16)
    g_out = dot("td,ctn->cdn", grad_hiddenb, attended)
    grad_att = dot("td,cdn->ctn", grad_hiddenb, w_o).astype(jnp.bfloat16)
    grad_att_h = grad_att.reshape(n_col, own, S, heads, HD).transpose(0, 1, 3, 2, 4)
    grad_att_h = grad_att_h.reshape(n_col * own * heads, S, HD)
    row_dot = jnp.sum(
        grad_att_h.astype(jnp.float32) * attended_h.astype(jnp.float32), -1, keepdims=True
    )
    grad_prob = dot("bqe,bke->bqk", grad_att_h, values)
    grad_scores = (prob * (grad_prob - row_dot)).astype(jnp.bfloat16)
    grad_q = dot("bqk,bke->bqe", grad_scores, keys) * scaling
    grad_k = dot("bqk,bqe->bke", grad_scores, queries) * scaling
    grad_v = dot("bqk,bqe->bke", probb, grad_att_h)

    def bias_sum(per_head):
        part = jnp.sum(per_head.reshape(n_col, own, heads, S, HD), (1, 3))
        return part.reshape(-1)

    grad_qkvb = jnp.concatenate(
        [merge(part.astype(jnp.bfloat16)) for part in (grad_q, grad_k, grad_v)], 2
    )
    g_in = dot("td,ctn->cdn", normed1, grad_qkvb)
    g_attn = scatter_grad(jnp.concatenate([g_in, g_out], 2))
    grad_n1 = dot("ctn,cdn->td", grad_qkvb, w_in)
    input_grad = grad_hidden + norm_backprop(grad_n1, xhat1, rstd1, gain1)
    input_grad_out = from_rows(input_grad, own)

    small = jnp.concatenate(
        [
            jnp.sum(grad_hidden, 0),
            jnp.sum(grad_n1 * xhat1, 0),
            jnp.sum(grad_n1, 0),
            jnp.sum(grad_n2 * xhat2, 0),
            jnp.sum(grad_n2, 0),
            jnp.sum(grad_y, 0),
            bias_sum(grad_q),
            bias_sum(grad_v),
            jnp.sum(grad_pre, 1).reshape(-1),
        ]
    )
    small = lax.psum(small, ("dp", "row", "col"))
    row_own = lax.dynamic_slice_in_dim(
        small[: 6 * D].reshape(6, D), row_idx * width_rows, width_rows, 1
    )
    qv_own = lax.dynamic_slice_in_dim(
        small[6 * D : 8 * D].reshape(2, D), col_idx * col_width, col_width, 1
    )
    up_own = lax.dynamic_slice_in_dim(small[8 * D :], col_idx * col_hidden, col_hidden, 0)
    grad_w_qkv = g_attn[:, : 3 * col_width].reshape(width_rows, 3, col_width).transpose(1, 0, 2)
    return (
        result_out,
        input_grad_out,
        grad_w_qkv,
        qv_own,
        g_attn[:, 3 * col_width :].T,
        row_own[0],
        row_own[1],
        row_own[2],
        row_own[3],
        row_own[4],
        g_up,
        up_own,
        g_down,
        row_own[5],
    )


def solution(mesh):
    return jax.shard_map(
        per_device,
        mesh=mesh,
        in_specs=(
            P("row", ("dp", "col")),
            P("dp"),
            P(None, "row", "col"),
            P(None, "col"),
            P("col", "row"),
            P("row"),
            P("row"),
            P("row"),
            P("row"),
            P("row"),
            P("row", "col"),
            P("col"),
            P("row", "col"),
            P("row"),
            P("row", ("dp", "col")),
        ),
        out_specs=(
            P("row", ("dp", "col")),
            P("row", ("dp", "col")),
            P(None, "row", "col"),
            P(None, "col"),
            P("col", "row"),
            P("row"),
            P("row"),
            P("row"),
            P("row"),
            P("row"),
            P("row", "col"),
            P("col"),
            P("row", "col"),
            P("row"),
        ),
        check_vma=False,
    )
```

```python
import math

import jax
import jax.numpy as jnp
from jax import lax
from jax.sharding import PartitionSpec as P

D = 768
HD = 64
FF = 3072
S = 197


EPS = 1e-06
ROOT_HALF = 0.7071067811865476
INV_ROOT_TAU = 0.3989422804014327


def gelu_value(preact):
    return 0.5 * preact * (1.0 + lax.erf(preact * ROOT_HALF))


def gelu_slope(preact):
    return (
        0.5 * (1.0 + lax.erf(preact * ROOT_HALF))
        + preact * jnp.exp(-0.5 * preact * preact) * INV_ROOT_TAU
    )


def norm_apply(features, gain_vec, shift_vec):
    average = jnp.sum(features, -1, keepdims=True) / D
    squares = jnp.sum(features * features, -1, keepdims=True) / D
    inv_std = lax.rsqrt(squares - average * average + EPS)
    centred = (features - average) * inv_std
    return (centred, inv_std, (centred * gain_vec + shift_vec).astype(jnp.bfloat16))


def norm_backprop(grad_normed, centred, inv_std, gain_vec):
    scaled = grad_normed * gain_vec
    totals = jnp.sum(scaled, -1, keepdims=True) / D
    mixture = jnp.sum(scaled * centred, -1, keepdims=True) / D
    return inv_std * (scaled - totals - centred * mixture)


def dot(spec, left, right):
    return jnp.einsum(spec, left, right, preferred_element_type=jnp.float32)


def swap(values, axis, bit):
    size = lax.axis_size(axis)
    return lax.ppermute(values, axis, [(i, i ^ bit) for i in range(size)])


def bits_of(axis):
    size = lax.axis_size(axis)
    assert size & (size - 1) == 0
    return [1 << b for b in reversed(range(size.bit_length() - 1))]


def gather_relative(block):
    entries = {0: block}
    for bit in bits_of("col"):
        arrived = {k | bit: swap(v, "col", bit) for k, v in entries.items()}
        entries.update(arrived)
    return [entries[k] for k in range(lax.axis_size("col"))]


def gather_weight(block):
    column = lax.all_gather(block, "row", axis=0, tiled=True)
    return jnp.stack(gather_relative(column))


def sum_everywhere(values, axes):
    for axis in axes:
        for bit in bits_of(axis):
            values = values + swap(values, axis, bit)
    return values


def scatter_grad(grad):
    parts = {k: grad[k] for k in range(grad.shape[0])}
    for bit in reversed(bits_of("col")):
        kept = {k: v for k, v in parts.items() if not k & bit}
        for k in kept:
            arrived = swap(parts[k | bit], "col", bit)
            total = kept[k].astype(jnp.float32) + arrived.astype(jnp.float32)
            kept[k] = total.astype(jnp.bfloat16)
        parts = kept
    part = lax.psum_scatter(parts[0], "row", scatter_dimension=0, tiled=True)
    if lax.axis_size("dp") == 2:
        other = swap(part, "dp", 1)
        return part.astype(jnp.float32) + other.astype(jnp.float32)
    return lax.psum(part.astype(jnp.float32), "dp")


def to_rows(flat, own, width_rows):
    tokens = flat.reshape(-1, S, width_rows)
    moved = lax.all_to_all(tokens, "row", split_axis=0, concat_axis=2, tiled=True)
    return moved.reshape(own * S, D)


def from_rows(values, own):
    moved = lax.all_to_all(
        values.astype(jnp.bfloat16).reshape(own, S, D),
        "row",
        split_axis=2,
        concat_axis=0,
        tiled=True,
    )
    return moved.astype(jnp.float32).reshape(1, -1)


def per_device(
    inputs,
    live_images,
    w_qkv,
    qv_bias,
    w_out,
    out_bias,
    attention_norm_gain,
    attention_norm_bias,
    feedforward_norm_gain,
    feedforward_norm_bias,
    w_up,
    up_bias,
    w_down,
    down_bias,
    cotangent,
):
    scaling = 1.0 / math.sqrt(HD)
    n_row, n_col = lax.axis_size("row"), lax.axis_size("col")
    row_idx, col_idx = lax.axis_index("row"), lax.axis_index("col")
    width_rows = D // n_row
    col_width = qv_bias.shape[1]
    col_hidden = up_bias.shape[0]
    heads = col_width // HD
    local_images = inputs.shape[1] // (S * width_rows)
    own = local_images // n_row
    rows = own * S

    tokens = to_rows(inputs, own, width_rows).astype(jnp.float32)
    w_attn = jnp.concatenate(
        [w_qkv.transpose(1, 0, 2).reshape(width_rows, 3 * col_width), w_out.T], 1
    )
    row_vecs = jnp.stack(
        [
            out_bias,
            attention_norm_gain,
            attention_norm_bias,
            feedforward_norm_gain,
            feedforward_norm_bias,
            down_bias,
        ]
    )
    placed = lax.dynamic_update_slice_in_dim(
        jnp.zeros((6, D), jnp.float32), row_vecs, row_idx * width_rows, 1
    )
    row_vecs = sum_everywhere(placed, ("row",))
    out_b, gain1, shift1, gain2, shift2, down_b = [row_vecs[i] for i in range(6)]
    col_vecs = jnp.stack(gather_relative(jnp.concatenate([qv_bias.reshape(-1), up_bias])))
    q_bias = col_vecs[:, :col_width]
    v_bias = col_vecs[:, col_width : 2 * col_width]
    up_b = col_vecs[:, 2 * col_width :]

    wa = gather_weight(w_attn)
    wu = gather_weight(w_up)
    wd = gather_weight(w_down)
    w_in, w_o = wa[:, :, : 3 * col_width], wa[:, :, 3 * col_width :]

    xhat1, rstd1, normed1 = norm_apply(tokens, gain1, shift1)
    cotangent, normed1 = lax.optimization_barrier((cotangent, normed1))
    cot = to_rows(cotangent, own, width_rows).astype(jnp.float32)
    first_image = col_idx * local_images + row_idx * own
    alive = (first_image + jnp.arange(own) < live_images[0]).astype(jnp.float32)
    grad_y = (cot.reshape(own, S, D) * alive[:, None, None]).reshape(rows, D)
    grad_yb = grad_y.astype(jnp.bfloat16)

    qkv_bias = jnp.concatenate([q_bias, jnp.zeros_like(q_bias), v_bias], 1)
    qkv = (dot("td,cdn->ctn", normed1, w_in) + qkv_bias[:, None, :]).astype(jnp.bfloat16)
    qkv = qkv.reshape(n_col, own, S, 3, heads, HD).transpose(3, 0, 1, 4, 2, 5)
    queries, keys, values = [qkv[i].reshape(n_col * own * heads, S, HD) for i in range(3)]
    scores = dot("bqe,bke->bqk", queries, keys) * scaling
    row_max = jnp.max(scores, -1, keepdims=True)
    log_total = row_max + jnp.log(jnp.sum(jnp.exp(scores - row_max), -1, keepdims=True))
    prob = jnp.exp(scores - log_total)
    probb = prob.astype(jnp.bfloat16)
    attended_h = dot("bqk,bke->bqe", probb, values).astype(jnp.bfloat16)

    def merge(per_head):
        out = per_head.reshape(n_col, own, heads, S, HD).transpose(0, 1, 3, 2, 4)
        return out.reshape(n_col, rows, col_width)

    attended = merge(attended_h)
    hidden = tokens + dot("ctn,cdn->td", attended, w_o) + out_b
    xhat2, rstd2, normed2 = norm_apply(hidden, gain2, shift2)
    preact = dot("td,cdf->ctf", normed2, wu) + up_b[:, None, :]
    activ = gelu_value(preact).astype(jnp.bfloat16)
    result = hidden + dot("ctf,cdf->td", activ, wd) + down_b
    result_out = from_rows(result, own)

    part_down = dot("td,ctf->cdf", grad_yb, activ).astype(jnp.bfloat16)
    grad_pre = dot("td,cdf->ctf", grad_yb, wd) * gelu_slope(preact)
    grad_preb = grad_pre.astype(jnp.bfloat16)
    part_down, grad_preb = lax.optimization_barrier((part_down, grad_preb))
    g_down = scatter_grad(part_down)
    part_up = dot("td,ctf->cdf", normed2, grad_preb).astype(jnp.bfloat16)
    grad_n2 = dot("ctf,cdf->td", grad_preb, wu)
    grad_hidden = grad_y + norm_backprop(grad_n2, xhat2, rstd2, gain2)
    grad_hiddenb = grad_hidden.astype(jnp.bfloat16)
    part_up, grad_hiddenb = lax.optimization_barrier((part_up, grad_hiddenb))
    g_up = scatter_grad(part_up)
    g_out = dot("td,ctn->cdn", grad_hiddenb, attended)
    grad_att = dot("td,cdn->ctn", grad_hiddenb, w_o).astype(jnp.bfloat16)
    grad_att_h = grad_att.reshape(n_col, own, S, heads, HD).transpose(0, 1, 3, 2, 4)
    grad_att_h = grad_att_h.reshape(n_col * own * heads, S, HD)
    row_dot = jnp.sum(
        grad_att_h.astype(jnp.float32) * attended_h.astype(jnp.float32), -1, keepdims=True
    )
    grad_prob = dot("bqe,bke->bqk", grad_att_h, values)
    grad_scores = (prob * (grad_prob - row_dot)).astype(jnp.bfloat16)
    grad_q = dot("bqk,bke->bqe", grad_scores, keys) * scaling
    grad_k = dot("bqk,bqe->bke", grad_scores, queries) * scaling
    grad_v = dot("bqk,bqe->bke", probb, grad_att_h)

    def bias_sum(per_head):
        part = jnp.sum(per_head.reshape(n_col, own, heads, S, HD), (1, 3))
        return part.reshape(n_col, col_width)

    grad_qkvb = jnp.concatenate(
        [merge(part.astype(jnp.bfloat16)) for part in (grad_q, grad_k, grad_v)], 2
    )
    g_in = dot("td,ctn->cdn", normed1, grad_qkvb)
    part_attn = jnp.concatenate([g_in, g_out], 2).astype(jnp.bfloat16)
    part_attn, grad_qkvb = lax.optimization_barrier((part_attn, grad_qkvb))
    g_attn = scatter_grad(part_attn)
    grad_n1 = dot("ctn,cdn->td", grad_qkvb, w_in)
    input_grad = grad_hidden + norm_backprop(grad_n1, xhat1, rstd1, gain1)
    input_grad_out = from_rows(input_grad, own)

    col_small = jnp.concatenate(
        [bias_sum(grad_q), bias_sum(grad_v), jnp.sum(grad_pre, 1)], 1
    )
    parts = {k: col_small[k] for k in range(n_col)}
    for bit in reversed(bits_of("col")):
        parts = {k: v + swap(parts[k | bit], "col", bit) for k, v in parts.items() if not k & bit}
    col_own = sum_everywhere(parts[0], ("row", "dp"))
    qv_own = col_own[: 2 * col_width].reshape(2, col_width)
    up_own = col_own[2 * col_width :]
    row_small = jnp.stack(
        [
            jnp.sum(grad_hidden, 0),
            jnp.sum(grad_n1 * xhat1, 0),
            jnp.sum(grad_n1, 0),
            jnp.sum(grad_n2 * xhat2, 0),
            jnp.sum(grad_n2, 0),
            jnp.sum(grad_y, 0),
        ]
    )
    row_small = sum_everywhere(row_small, ("col", "row", "dp"))
    row_own = lax.dynamic_slice_in_dim(row_small, row_idx * width_rows, width_rows, 1)
    grad_w_qkv = g_attn[:, : 3 * col_width].reshape(width_rows, 3, col_width).transpose(1, 0, 2)
    return (
        result_out,
        input_grad_out,
        grad_w_qkv,
        qv_own,
        g_attn[:, 3 * col_width :].T,
        row_own[0],
        row_own[1],
        row_own[2],
        row_own[3],
        row_own[4],
        g_up,
        up_own,
        g_down,
        row_own[5],
    )


def solution(mesh):
    return jax.shard_map(
        per_device,
        mesh=mesh,
        in_specs=(
            P("row", ("dp", "col")),
            P("dp"),
            P(None, "row", "col"),
            P(None, "col"),
            P("col", "row"),
            P("row"),
            P("row"),
            P("row"),
            P("row"),
            P("row"),
            P("row", "col"),
            P("col"),
            P("row", "col"),
            P("row"),
            P("row", ("dp", "col")),
        ),
        out_specs=(
            P("row", ("dp", "col")),
            P("row", ("dp", "col")),
            P(None, "row", "col"),
            P(None, "col"),
            P("col", "row"),
            P("row"),
            P("row"),
            P("row"),
            P("row"),
            P("row"),
            P("row", "col"),
            P("col"),
            P("row", "col"),
            P("row"),
        ),
        check_vma=False,
    )
```
